256 devices in a mesh: kv: 4 (over y), seq: 64 (over z, x, core).
Axes of the slice: x: 4, y: 4, z: 8, core: 2. Of those that a mesh axis runs over, the one named last changes fastest.
Arguments:
- queries: bfloat16 [4096, 4, 8192], P('seq', 'kv'), may hold values from -41 to 41
- key_state_rows: bfloat16 [4096, 4, 1024], P('seq', 'kv'), may hold values from -6 to 6
- value_state_rows: bfloat16 [4096, 4, 1024], P('seq', 'kv'), may hold values from -6 to 6
- output_gradient: bfloat16 [16384, 8192], P('seq', 'kv'), may hold values from -6 to 6
- parents: int32 [128], replicated, may hold values from -1 to 126, as said below
Outputs:
- attended: bfloat16 [16384, 8192], P('seq', 'kv')
- query_grad: bfloat16 [4096, 4, 8192], P('seq', 'kv')
- key_gradient_rows: bfloat16 [4096, 4, 1024], P('seq', 'kv')
- value_gradient_rows: bfloat16 [4096, 4, 1024], P('seq', 'kv')
The draws below stay inside these ranges and needn't reach their ends.
Inputs may be any that keep to these rules, and one draw needn't show every extreme that they name: parents[b] is -1 for a tree's root and otherwise a block of the same tree below b. The blocks of a tree are consecutive, a tree begins at the first block of a device and covers at most 5 consecutive devices, so every ancestor of block b lies at block 2 * (b // 2 - 4) or above; in every draw some tree covers 4 + 1 devices.
All inputs are finite; a program needn't handle non-finite values.
Results may differ from the reference program's by a relative error of at most 0.034.
Values may be sent and summed in bfloat16 or wider, within the bound.
No kernel may reach another device: no remote copies, remote signals or barrier semaphores. Data moves between devices by JAX's collectives and lax.ppermute only.
A program may use at most 64 MiB of HBM per device.

```python
import math
import jax
import jax.numpy as jnp
from jax import lax

QUERY_HEADS = 64
KEY_VALUE_HEADS = 8
HEAD_WIDTH = 128
BLK = 128
REACH = 4
BLK_DEV = 2
TREE_TOKENS = 16384
BLOCKS = 128
N_KV = 4


def drawn_pair(key):
    base_key = jax.random.fold_in(key, 7)
    query_random_key, state_random_key = jax.random.split(base_key, 2)
    heads_per_group = QUERY_HEADS // KEY_VALUE_HEADS
    state_rows = jnp.clip(jax.random.normal(state_random_key, (TREE_TOKENS, KEY_VALUE_HEADS, HEAD_WIDTH), jnp.float32), -6.0, 6.0)
    queries = jnp.clip(jax.random.normal(query_random_key, (TREE_TOKENS, KEY_VALUE_HEADS, heads_per_group, HEAD_WIDTH), jnp.float32), -6.0, 6.0)
    return (queries, state_rows)


def draw_queries(key, part):
    queries, state_rows = drawn_pair(key)
    return queries.reshape(TREE_TOKENS // N_KV, N_KV, QUERY_HEADS * HEAD_WIDTH).astype(jnp.bfloat16)


def draw_key_state_rows(key, part):
    queries, state_rows = drawn_pair(key)
    return state_rows.reshape(TREE_TOKENS // N_KV, N_KV, KEY_VALUE_HEADS * HEAD_WIDTH).astype(jnp.bfloat16)


def draw_parents(key, part):
    base_key = jax.random.fold_in(key, 11)
    span_key, follow_key, offset_key = jax.random.split(base_key, 3)
    device_count = BLOCKS // BLK_DEV
    tree_span = jax.random.randint(span_key, (device_count,), 1, REACH + 2)
    tree_span = tree_span.at[0].set(REACH + 1)
    tree_first = jnp.cumsum(tree_span) - tree_span
    device_ids = jnp.arange(device_count, dtype=jnp.int32)
    starts = jnp.any(tree_first[:, None] == device_ids[None, :], axis=0)
    tree_start = lax.cummax(jnp.where(starts, device_ids, 0), axis=0)
    block_ids = jnp.arange(BLOCKS, dtype=jnp.int32)
    lowest = tree_start[block_ids // BLK_DEV] * BLK_DEV
    follow = jax.random.randint(follow_key, (BLOCKS,), 0, 2) == 0
    offset = jax.random.randint(offset_key, (BLOCKS,), 0, jnp.maximum(block_ids - lowest, 1))
    chosen_parent = jnp.where(follow, block_ids - 1, lowest + offset)
    return jnp.where(block_ids == lowest, -1, chosen_parent).astype(jnp.int32)


def steps_of(key, shape, cuts, smallest, high):
    factor_of = 1.0
    for dim, shards_of in cuts:
        draws = jax.random.uniform(jax.random.fold_in(jax.random.fold_in(key, 6), dim), (shards_of,), jnp.float32, smallest / len(cuts), high / len(cuts))
        factor_of = factor_of * jnp.repeat(jnp.exp(draws), shape[dim] // shards_of).reshape((-1,) + (1,) * (len(shape) - 1 - dim))
    return factor_of


def bell_draw(key, extent, width, bound, shards=(), kind=jnp.bfloat16):
    entries = jax.random.normal(key, extent, jnp.float32) * width
    if len(shards) > 0:
        entries = steps_of(key, extent, shards, -0.22, 0.18) * entries
    return jnp.clip(entries, min=-bound, max=bound).astype(kind)


def setup_inputs(seed: int = 0) -> dict:
    key_list = jax.random.split(jax.random.key(seed), 6)
    queries = draw_queries(jax.random.fold_in(key_list[5], 71), 0)
    key_state_rows = draw_key_state_rows(jax.random.fold_in(key_list[5], 71), 0)
    value_state_rows = bell_draw(key_list[2], (TREE_TOKENS // N_KV, N_KV, KEY_VALUE_HEADS * HEAD_WIDTH), 1.0, 6.0, ((0, 64), (1, 4)))
    output_gradient = bell_draw(key_list[3], (TREE_TOKENS, QUERY_HEADS * HEAD_WIDTH), 1.0, 6.0, ((0, 64), (1, 4)))
    parents = draw_parents(jax.random.fold_in(key_list[5], 71), 0)
    return {"queries": queries, "key_state_rows": key_state_rows, "value_state_rows": value_state_rows, "output_gradient": output_gradient, "parents": parents}


LOW_LOGIT = -1e+30

def ancestor_table(parents):
    block_ids = jnp.arange(BLOCKS, dtype=jnp.int32)
    table = jnp.zeros((BLOCKS, BLOCKS), dtype=bool)
    current = parents.astype(jnp.int32)
    for level in range(BLK_DEV * (REACH + 1)):
        table = table | (current[:, None] == block_ids[None, :]) & (current[:, None] >= 0)
        current = jnp.where(current >= 0, parents[jnp.maximum(current, 0)], -1).astype(jnp.int32)
    return table

def reference(queries, key_state_rows, value_state_rows, output_gradient, parents):
    heads_per_group = QUERY_HEADS // KEY_VALUE_HEADS
    inverse_root = 1.0 / math.sqrt(HEAD_WIDTH)
    window_tokens = BLK_DEV * (REACH + 1) * BLK
    query_everything = queries.reshape(TREE_TOKENS, KEY_VALUE_HEADS, heads_per_group, HEAD_WIDTH)
    key_everything = key_state_rows.reshape(TREE_TOKENS, KEY_VALUE_HEADS, HEAD_WIDTH)
    value_everything = value_state_rows.reshape(TREE_TOKENS, KEY_VALUE_HEADS, HEAD_WIDTH)
    gradient_everything = output_gradient.reshape(TREE_TOKENS, KEY_VALUE_HEADS, heads_per_group, HEAD_WIDTH)
    table = ancestor_table(parents)
    query_position = jnp.arange(BLK, dtype=jnp.int32)

    def one_block(running, q_block):
        key_gradients, value_gradients = running
        device = q_block // BLK_DEV
        start_blk = (jnp.maximum(device - REACH, 0) * BLK_DEV).astype(jnp.int32)
        start = (start_blk * BLK).astype(jnp.int32)
        row_start = (q_block * BLK).astype(jnp.int32)
        q_tile = lax.dynamic_slice_in_dim(query_everything, row_start, BLK, 0).astype(jnp.float32)
        g_tile = lax.dynamic_slice_in_dim(gradient_everything, row_start, BLK, 0).astype(jnp.float32)
        key_window = lax.dynamic_slice_in_dim(key_everything, start, window_tokens, 0).astype(jnp.float32)
        value_window = lax.dynamic_slice_in_dim(value_everything, start, window_tokens, 0).astype(jnp.float32)
        key_block = start_blk + jnp.arange(window_tokens, dtype=jnp.int32) // BLK
        key_position = jnp.arange(window_tokens, dtype=jnp.int32) % BLK
        linked = table[q_block][key_block]
        same_block = key_block == q_block
        allowed = linked[None, :] | same_block[None, :] & (key_position[None, :] <= query_position[:, None])
        logits = jnp.einsum('ihgd,jhd->hgij', q_tile, key_window) * inverse_root
        row_peak = lax.optimization_barrier(jnp.max(jnp.where(allowed, logits, LOW_LOGIT), axis=-1))
        expsum = lax.optimization_barrier(jnp.sum(jnp.where(allowed, jnp.exp(logits - row_peak[..., None]), 0.0), axis=-1))
        log_total = row_peak + jnp.log(expsum)
        exact_probs = jnp.where(allowed, jnp.exp(logits - log_total[..., None]), 0.0)
        rounded_probs = lax.optimization_barrier(exact_probs.astype(jnp.bfloat16)).astype(jnp.float32)
        attended = jnp.einsum('hgij,jhd->ihgd', rounded_probs, value_window).astype(jnp.bfloat16)
        row_dot = jnp.einsum('ihgd,ihgd->hgi', g_tile, attended.astype(jnp.float32))
        dprobs = jnp.einsum('ihgd,jhd->hgij', g_tile, value_window)
        dlogits = exact_probs * (dprobs - row_dot[..., None]) * inverse_root
        dlogits = lax.optimization_barrier(dlogits.astype(jnp.bfloat16)).astype(jnp.float32)
        query_part = jnp.einsum('hgij,jhd->ihgd', dlogits, key_window).astype(jnp.bfloat16)
        key_part = jnp.einsum('hgij,ihgd->jhd', dlogits, q_tile)
        value_part = jnp.einsum('hgij,ihgd->jhd', rounded_probs, g_tile)
        old_keys = lax.dynamic_slice_in_dim(key_gradients, start, window_tokens, 0)
        key_gradients = lax.dynamic_update_slice_in_dim(key_gradients, old_keys + key_part, start, 0)
        old_values = lax.dynamic_slice_in_dim(value_gradients, start, window_tokens, 0)
        value_gradients = lax.dynamic_update_slice_in_dim(value_gradients, old_values + value_part, start, 0)
        return ((key_gradients, value_gradients), (attended, query_part))
    zero_key_values = jnp.zeros((TREE_TOKENS, KEY_VALUE_HEADS, HEAD_WIDTH), jnp.float32)
    (key_gradients, value_gradients), (attended, query_part) = lax.scan(one_block, (zero_key_values, zero_key_values), jnp.arange(BLOCKS, dtype=jnp.int32))
    attended = attended.reshape(TREE_TOKENS, QUERY_HEADS * HEAD_WIDTH)
    query_grad = query_part.reshape(TREE_TOKENS // N_KV, N_KV, QUERY_HEADS * HEAD_WIDTH)
    key_gradient_rows = key_gradients.astype(jnp.bfloat16).reshape(TREE_TOKENS // N_KV, N_KV, KEY_VALUE_HEADS * HEAD_WIDTH)
    value_gradient_rows = value_gradients.astype(jnp.bfloat16).reshape(TREE_TOKENS // N_KV, N_KV, KEY_VALUE_HEADS * HEAD_WIDTH)
    return (attended, query_grad, key_gradient_rows, value_gradient_rows)
```

```python
import functools
import math

import jax
import jax.numpy as jnp
from jax import lax
from jax.experimental import pallas as pl
from jax.experimental.pallas import tpu as pltpu
from jax.sharding import PartitionSpec as P

QUERY_HEADS = 64
KEY_VALUE_HEADS = 8
D = 128
BLK = 128
REACH = 4
N_KV = 4
LOCAL_KV = KEY_VALUE_HEADS // N_KV
GROUP = QUERY_HEADS // KEY_VALUE_HEADS
BLOCKS_HERE = 2
WINDOW = BLOCKS_HERE * (REACH + 1)
ROWS = GROUP * BLK
R_BLK = BLK // N_KV
QW = LOCAL_KV * GROUP * D
KW = LOCAL_KV * D
LOW_LOGIT = -1e30
SCALE = 1.0 / math.sqrt(D)
F32 = jnp.float32
BF16 = jnp.bfloat16
NN = (((1,), (0,)), ((), ()))
NT = (((1,), (1,)), ((), ()))


def mm(a, b, dims=NN):
    return lax.dot_general(a, b, dims, preferred_element_type=F32)


def passed_along(value, axis, by):
    devices = lax.axis_size(axis)
    pairs = [(i, i + by) for i in range(devices) if 0 <= i + by < devices]
    return lax.ppermute(value, axis, pairs)


def pack_kernel(q_ref, k_ref, v_ref, qx_ref, kvx_ref):
    for c in range(N_KV):
        qx_ref[c] = q_ref[:, c * QW : (c + 1) * QW]
        kvx_ref[c, :, :KW] = k_ref[:, c * KW : (c + 1) * KW]
        kvx_ref[c, :, KW:] = v_ref[:, c * KW : (c + 1) * KW]


def attention_kernel(
    parents, place, q_ref, kv0, kv1, kv2, kv3, kv4, g_ref,
    att_ref, dq_ref, p0, p1, p2, p3, p4,
    kw, vw, dkt, dvt, qs, qt, gs, gt, probs, o_acc, dq_acc, row, tot, perm, bias, path, depth,
):
    first = (place[0] - REACH) * BLOCKS_HERE
    for qb in range(BLOCKS_HERE):
        path[qb, 0] = REACH * BLOCKS_HERE + qb

        def climb(unused, state):
            current, count = state
            above = parents[jnp.maximum(current, 0)]
            found = jnp.logical_and(current >= 0, above >= 0)

            @pl.when(found)
            def _():
                path[qb, count] = jnp.clip(above - first, 0, WINDOW - 1)

            return (jnp.where(found, above, -1), count + found.astype(jnp.int32))

        depth[qb] = lax.fori_loop(
            0, WINDOW - 1, climb, (place[0] * BLOCKS_HERE + qb, jnp.int32(1))
        )[1]

    fetched = (kv4, kv3, kv2, kv1, kv0)
    for w in range(WINDOW):
        source = fetched[w // BLOCKS_HERE]
        r0 = (w % BLOCKS_HERE) * R_BLK
        for k in range(N_KV):
            for h in range(LOCAL_KV):
                kw[w, h, k * R_BLK : (k + 1) * R_BLK, :] = source[
                    k, r0 : r0 + R_BLK, h * D : (h + 1) * D
                ]
                vw[w, h, k * R_BLK : (k + 1) * R_BLK, :] = source[
                    k, r0 : r0 + R_BLK, KW + h * D : KW + (h + 1) * D
                ]
    dkt[...] = jnp.zeros_like(dkt)
    dvt[...] = jnp.zeros_like(dvt)
    i0 = lax.broadcasted_iota(jnp.int32, (BLK, BLK), 0)
    i1 = lax.broadcasted_iota(jnp.int32, (BLK, BLK), 1)

    def position(i):
        return N_KV * (i % R_BLK) + i // R_BLK

    perm[0] = (position(i0) == i1).astype(F32).astype(BF16)
    perm[1] = (position(i1) == i0).astype(F32).astype(BF16)
    bias[0] = jnp.where(position(i0) >= position(i1), 0.0, LOW_LOGIT)
    bias[1] = jnp.zeros((BLK, BLK), F32)

    def one(step, carry):
        qb = step // LOCAL_KV
        h = step % LOCAL_KV
        cols = pl.ds(pl.multiple_of(h * ROWS, ROWS), ROWS)
        q_rows = pl.ds(pl.multiple_of(qb * R_BLK, R_BLK), R_BLK)
        g_rows = pl.ds(pl.multiple_of(qb * BLK, BLK), BLK)
        n = depth[qb]
        for k in range(N_KV):
            part = q_ref[k, q_rows, cols]
            for j in range(GROUP):
                qs[j * BLK + k * R_BLK : j * BLK + (k + 1) * R_BLK, :] = part[
                    :, j * D : (j + 1) * D
                ]
        g_all = mm(perm[0], g_ref[g_rows, cols]).astype(BF16)
        for j in range(GROUP):
            gs[j * BLK : (j + 1) * BLK, :] = g_all[:, j * D : (j + 1) * D]
            gt[:, j * BLK : (j + 1) * BLK] = g_all[:, j * D : (j + 1) * D].T
            qt[:, j * BLK : (j + 1) * BLK] = qs[j * BLK : (j + 1) * BLK, :].T
        row[...] = jnp.full_like(row, LOW_LOGIT)

        def score(i, c):
            tile = mm(qs[...], kw[path[qb, i], h], NT) * SCALE
            tile = (
                tile.reshape(GROUP, BLK, BLK) + bias[jnp.minimum(i, 1)][None]
            ).reshape(ROWS, BLK)
            probs[i] = tile
            row[...] = jnp.maximum(row[...], tile)
            return c

        lax.fori_loop(0, n, score, 0)
        row[...] = jnp.broadcast_to(jnp.max(row[...], axis=1, keepdims=True), (ROWS, BLK))
        tot[...] = jnp.zeros_like(tot)

        def grow(i, c):
            tile = jnp.exp(probs[i] - row[...])
            probs[i] = tile
            tot[...] += tile
            return c

        lax.fori_loop(0, n, grow, 0)
        row[...] = jnp.broadcast_to(
            1.0 / jnp.sum(tot[...], axis=1, keepdims=True), (ROWS, BLK)
        )
        o_acc[...] = jnp.zeros_like(o_acc)

        def forward(i, c):
            w = path[qb, i]
            tile = probs[i] * row[...]
            probs[i] = tile
            weights = tile.astype(BF16)
            o_acc[...] += mm(weights, vw[w, h])
            dvt[w, h] += mm(gt[...], weights)
            return c

        lax.fori_loop(0, n, forward, 0)
        attended = o_acc[...].astype(BF16)
        row[...] = jnp.broadcast_to(
            jnp.sum(gs[...].astype(F32) * attended.astype(F32), axis=1, keepdims=True),
            (ROWS, BLK),
        )
        side = jnp.concatenate(
            [attended[j * BLK : (j + 1) * BLK, :] for j in range(GROUP)], axis=1
        )
        att_ref[g_rows, cols] = mm(perm[1], side).astype(BF16)
        dq_acc[...] = jnp.zeros_like(dq_acc)

        def backward(i, c):
            w = path[qb, i]
            dprobs = mm(gs[...], vw[w, h], NT)
            dlogits = (probs[i] * (dprobs - row[...]) * SCALE).astype(BF16)
            dq_acc[...] += mm(dlogits, kw[w, h])
            dkt[w, h] += mm(qt[...], dlogits)
            return c

        lax.fori_loop(0, n, backward, 0)
        dq = dq_acc[...].astype(BF16)
        for k in range(N_KV):
            dq_ref[k, q_rows, cols] = jnp.concatenate(
                [dq[j * BLK + k * R_BLK : j * BLK + (k + 1) * R_BLK, :] for j in range(GROUP)],
                axis=1,
            )
        return carry

    lax.fori_loop(0, BLOCKS_HERE * LOCAL_KV, one, 0)
    partial = (p4, p3, p2, p1, p0)
    for w in range(WINDOW):
        target = partial[w // BLOCKS_HERE]
        r0 = (w % BLOCKS_HERE) * R_BLK
        for h in range(LOCAL_KV):
            dk = dkt[w, h].T.astype(target.dtype)
            dv = dvt[w, h].T.astype(target.dtype)
            for k in range(N_KV):
                target[k, r0 : r0 + R_BLK, h * D : (h + 1) * D] = dk[k * R_BLK : (k + 1) * R_BLK]
                target[k, r0 : r0 + R_BLK, KW + h * D : KW + (h + 1) * D] = dv[
                    k * R_BLK : (k + 1) * R_BLK
                ]


def unpack_kernel(x_ref, o_ref):
    for c in range(N_KV):
        o_ref[:, c * QW : (c + 1) * QW] = x_ref[c]


def unpack_pair_kernel(x_ref, k_ref, v_ref):
    for c in range(N_KV):
        k_ref[:, c * KW : (c + 1) * KW] = x_ref[c, :, :KW]
        v_ref[:, c * KW : (c + 1) * KW] = x_ref[c, :, KW:]


def exchange(x):
    return lax.all_to_all(x, "kv", split_axis=0, concat_axis=0, tiled=True)


def local(queries, key_state_rows, value_state_rows, output_gradient, parents):
    rows = queries.shape[0]
    shape = jax.ShapeDtypeStruct
    qx, kvx = pl.pallas_call(
        pack_kernel,
        out_shape=(shape((N_KV, rows, QW), BF16), shape((N_KV, rows, 2 * KW), BF16)),
        name="pack",
    )(queries.reshape(rows, -1), key_state_rows.reshape(rows, -1), value_state_rows.reshape(rows, -1))
    own = exchange(kvx)
    q_heads = exchange(qx)
    fetched = [own] + [passed_along(own, "seq", o) for o in range(1, REACH + 1)]
    place = lax.axis_index("seq").astype(jnp.int32).reshape(1)
    vmem = pl.BlockSpec(memory_space=pltpu.VMEM)
    smem = pl.BlockSpec(memory_space=pltpu.SMEM)
    part = (N_KV, rows, 2 * KW)
    attended, dqx, *partials = pl.pallas_call(
        attention_kernel,
        in_specs=[smem, smem] + [vmem] * 7,
        out_specs=[vmem] * 7,
        out_shape=[
            shape(output_gradient.shape, BF16),
            shape((N_KV, rows, QW), BF16),
            shape(part, F32),
        ]
        + [shape(part, BF16)] * REACH,
        scratch_shapes=[
            pltpu.VMEM((WINDOW, LOCAL_KV, BLK, D), BF16),
            pltpu.VMEM((WINDOW, LOCAL_KV, BLK, D), BF16),
            pltpu.VMEM((WINDOW, LOCAL_KV, D, BLK), F32),
            pltpu.VMEM((WINDOW, LOCAL_KV, D, BLK), F32),
            pltpu.VMEM((ROWS, D), BF16),
            pltpu.VMEM((D, ROWS), BF16),
            pltpu.VMEM((ROWS, D), BF16),
            pltpu.VMEM((D, ROWS), BF16),
            pltpu.VMEM((WINDOW, ROWS, BLK), F32),
            pltpu.VMEM((ROWS, D), F32),
            pltpu.VMEM((ROWS, D), F32),
            pltpu.VMEM((ROWS, BLK), F32),
            pltpu.VMEM((ROWS, BLK), F32),
            pltpu.VMEM((2, BLK, BLK), BF16),
            pltpu.VMEM((2, BLK, BLK), F32),
            pltpu.SMEM((BLOCKS_HERE, WINDOW), jnp.int32),
            pltpu.SMEM((BLOCKS_HERE,), jnp.int32),
        ],
        name="tree_attention",
    )(parents, place, q_heads, *fetched, output_gradient)
    summed = partials[0]
    for o in range(1, REACH + 1):
        summed = summed + passed_along(partials[o], "seq", -o).astype(F32)
    dkv = exchange(summed.astype(BF16))
    dq = exchange(dqx)
    query_out = pl.pallas_call(
        unpack_kernel, out_shape=shape((rows, N_KV * QW), BF16), name="unpack_queries"
    )(dq).reshape(queries.shape)
    key_out, value_out = pl.pallas_call(
        unpack_pair_kernel,
        out_shape=[shape((rows, N_KV * KW), BF16)] * 2,
        name="unpack_keys_values",
    )(dkv)
    return (
        attended,
        query_out,
        key_out.reshape(key_state_rows.shape),
        value_out.reshape(value_state_rows.shape),
    )


def solution(mesh):
    placed = (P("seq", "kv", None), P("seq", "kv", None), P("seq", "kv", None), P("seq", "kv"), P())
    return jax.shard_map(
        local,
        mesh=mesh,
        in_specs=placed,
        out_specs=(
            P("seq", "kv"),
            P("seq", "kv", None),
            P("seq", "kv", None),
            P("seq", "kv", None),
        ),
        check_vma=False,
    )
```
